128 devices in a mesh: node: 4 (over y_hi, core), hst: 32 (over y_lo, x, z).
Axes of the slice: x: 4, y: 4 (y_hi: 2, y_lo: 2; y = y_hi * 2 + y_lo), z: 4, core: 2. Of those that a mesh axis runs over, the one named last changes fastest.
Arguments:
- hidden: bfloat16 [32, 4096, 640], P('hst', 'node'), may hold values from -6 to 6
- cotangent: bfloat16 [32, 4096, 4608], P('hst', 'node'), may hold values from -12 to 12
- anchor: float32 [32, 640, 4608], P('hst', 'node'), may hold values from -0.25 to 0.25
- momentum: float32 [32, 640, 4608], P('hst', 'node'), may hold values from -0.6 to 0.6
- round_mask: int32 [1], replicated, may hold values from 1 to 31
Outputs:
- weights_out: bfloat16 [32, 640, 4608], P('hst')
- momentum_out: float32 [32, 640, 4608], P('hst', 'node')
The draws below stay inside these ranges and needn't reach their ends.
Inputs may be any that keep to these rules, and one draw needn't show every extreme that they name: round_mask is the same for all hosts; host i averages with the hosts i XOR s for every s whose bits lie within round_mask.
All inputs are finite; a program needn't handle non-finite values.
Results may differ from the reference program's by a relative error of at most 0.009.
Values may be sent and summed in bfloat16 or wider, within the bound.
A program may use at most 256 MiB of HBM per device.

```python
import jax
import jax.numpy as jnp
from jax import lax

D = 4608
H = 640
TOK_DEV = 1024
NODE_TOK = 4096
N_NODE = 4
N_HST = 32


def steps_of(rng, shape, shards, smallest, high):
    level, own = 1.0, jax.random.fold_in(rng, 6)
    for axis_at, shards_of in shards:
        steps = jnp.exp(jax.random.uniform(jax.random.fold_in(own, axis_at), (shards_of,), jnp.float32, smallest / len(shards), high / len(shards)))
        level = level * jnp.repeat(steps, shape[axis_at] // shards_of).reshape([-1 if axis == axis_at else 1 for axis in range(len(shape))])
    return level


def gaussian(stream_key, dims, width, reach, pieces=(), kind=jnp.bfloat16):
    factor_of = steps_of(stream_key, dims, pieces, -0.22, 0.18) if pieces else 1.0
    result = jax.random.normal(stream_key, dims, jnp.float32) * width * factor_of
    return jnp.minimum(jnp.maximum(result, -reach), reach).astype(kind)


def setup_inputs(seed: int = 0) -> dict:
    seeds = jax.random.split(jax.random.key(seed), 6)
    hidden = gaussian(seeds[0], (N_HST, NODE_TOK, H), 1.0, 6.0, ((0, 32), (1, 4)))
    cotangent = gaussian(seeds[1], (N_HST, NODE_TOK, D), 2.0, 12.0, ((0, 32), (1, 4)))
    anchor = gaussian(seeds[2], (N_HST, H, D), H ** -0.5, 0.25, ((0, 32), (1, 4)), jnp.float32)
    momentum = gaussian(seeds[3], (N_HST, H, D), 0.1, 0.6, ((0, 32), (1, 4)), jnp.float32)
    round_mask = jax.random.randint(seeds[4], (1,), 1, N_HST).astype(jnp.int32)
    return {"hidden": hidden, "cotangent": cotangent, "anchor": anchor, "momentum": momentum, "round_mask": round_mask}


base_rate = 0.5
slow_rate = 1.0
slow_beta = 0.7

def host_grad(inputs_pair):
    activations, cotangents = inputs_pair
    activations = activations.reshape(N_NODE, TOK_DEV, H)
    cotangents = cotangents.reshape(N_NODE, TOK_DEV, D)
    summed = jnp.zeros((H, D), jnp.float32)
    for device in range(N_NODE):
        product = jnp.dot(activations[device].T, cotangents[device], preferred_element_type=jnp.float32)
        product = product * (1.0 / (TOK_DEV * N_NODE))
        rounded = lax.optimization_barrier(product.astype(jnp.bfloat16))
        summed = summed + rounded.astype(jnp.float32)
    return summed

def reference(hidden, cotangent, anchor, momentum, round_mask):
    grads = lax.map(host_grad, (hidden, cotangent))
    stepped = anchor - base_rate * grads
    host_ids = jnp.arange(N_HST, dtype=jnp.int32)
    free_bits = jnp.bitwise_xor(round_mask[0], jnp.int32(N_HST - 1))
    mixing = (jnp.bitwise_and(jnp.bitwise_xor(host_ids[:, None], host_ids[None, :]), free_bits) == 0).astype(jnp.float32)
    mixing = mixing / lax.optimization_barrier(jnp.sum(mixing, axis=1, keepdims=True))
    averaged = jnp.tensordot(mixing, stepped, axes=1, precision=lax.Precision.HIGHEST)
    momentum_out = slow_beta * momentum + (anchor - averaged) / base_rate
    updated = anchor - slow_rate * base_rate * momentum_out
    return (updated.astype(jnp.bfloat16), momentum_out)
```

```python
import functools

import jax
import jax.numpy as jnp
from jax import lax
from jax.experimental import pallas as pl
from jax.experimental.pallas import tpu as pltpu
from jax.sharding import PartitionSpec as P

MESH = pl.DeviceIdType.MESH
BF16, F32 = jnp.bfloat16, jnp.float32

base_rate = 0.5
slow_rate = 1.0
slow_beta = 0.7

WIDTH = 256
LAG = 1


def kernel(bits, chunks, width, rows,
           hid, cot, anc, mom, wout, mout,
           hv, ht, cotv, ancv, momv, pb, cr, ys, yr, st, gs, gr, momo, wr,
           in_sem, cot_sem, out_sem, send_sem, recv_sem):
    node = lax.axis_index("node")
    hst = lax.axis_index("hst")
    core = lax.rem(node, 2)
    yh = lax.div(node, 2)
    oc = 1 - core
    oy = 1 - yh
    mate = (yh * 2 + oc, hst)
    across = (oy * 2 + core, hst)
    far = oy * 2 + core
    partners = []
    for b in bits:
        value = lax.rem(lax.div(hst, 1 << b), 2)
        partners.append((node, hst + (1 - 2 * value) * (1 << b)))
    nb = len(bits)
    K_CORE, K_Y, K_WY, K_WC, K_WR, K_G = 0, 1, 2, 3, 4, 5

    barrier = pltpu.get_barrier_semaphore()
    everyone = [mate, across] + partners
    for who in everyone:
        pl.semaphore_signal(barrier, inc=1, device_id=who, device_id_type=MESH)

    load_h = pltpu.make_async_copy(hid.at[0], hv, in_sem.at[0])
    load_a = pltpu.make_async_copy(anc.at[0], ancv, in_sem.at[1])
    load_m = pltpu.make_async_copy(mom.at[0], momv, in_sem.at[2])

    def cols(c):
        return pl.ds(pl.multiple_of(c * width, width), width)

    def row_block(n):
        return pl.ds(pl.multiple_of(n * rows, rows), rows)

    def load_cot(c):
        return pltpu.make_async_copy(cot.at[0, :, cols(c)], cotv.at[c], cot_sem.at[c])

    load_h.start()
    load_cot(0).start()
    load_cot(1).start()
    load_a.start()

    def start_cot(c, carry):
        load_cot(c).start()
        return carry

    lax.fori_loop(2, chunks, start_cot, 0)
    load_m.start()

    load_h.wait()
    for j in range(ht.shape[0] // 128):
        ht[pl.ds(j * 128, 128), :] = hv[:, pl.ds(j * 128, 128)].T
    load_a.wait()
    load_m.wait()
    pl.semaphore_wait(barrier, len(everyone))

    def remote(kind, c, src, dst, who):
        return pltpu.make_async_remote_copy(
            src_ref=src, dst_ref=dst, send_sem=send_sem.at[kind, c], recv_sem=recv_sem.at[kind, c],
            device_id=who, device_id_type=MESH)

    def core_copy(c):
        return remote(K_CORE, c, pb.at[c, :, oc], cr.at[c], mate)

    def y_copy(c):
        return remote(K_Y, c, ys.at[c], yr.at[c], across)

    def g_copy(i, c):
        return remote(K_G + i, c, gs.at[c], gr.at[i, c], partners[i])

    def wy_copy(c):
        return remote(K_WY, c, gs.at[c], wr.at[c], across)

    def wc_copy(c):
        return remote(K_WC, c, gs.at[c], wout.at[0, row_block(node), cols(c)], mate)

    def wr_copy(c):
        return remote(K_WR, c, wr.at[c], wout.at[0, row_block(far), cols(c)], mate)

    def own_out(c):
        return pltpu.make_async_copy(gs.at[c], wout.at[0, row_block(node), cols(c)], out_sem.at[0, c])

    def far_out(c):
        return pltpu.make_async_copy(wr.at[c], wout.at[0, row_block(far), cols(c)], out_sem.at[1, c])

    def mom_out(c):
        return pltpu.make_async_copy(momo.at[c], mout.at[0, :, cols(c)], out_sem.at[2, c])

    scale = -base_rate / (hid.shape[1] * 4)

    def stage_a(c):
        load_cot(c).wait()
        product = jnp.dot(ht[...], cotv[c], preferred_element_type=F32)
        pb[c] = (product * scale).astype(BF16).reshape(2, 2, rows, width)
        core_copy(c).start()

    def stage_b(c):
        core_copy(c).wait()
        ys[c] = (pb[c, oy, core].astype(F32) + cr[c, oy].astype(F32)).astype(BF16)
        y_copy(c).start()

    def stage_c(c):
        y_copy(c).wait()
        s = ancv[:, cols(c)] + (pb[c, yh, core].astype(F32) + cr[c, yh].astype(F32) + yr[c].astype(F32))
        st[c] = s
        gs[c] = s.astype(BF16)
        g_copy(0, c).start()

    def stage_g(i, c):
        g_copy(i, c).wait()
        s = 0.5 * (st[c] + gr[i, c].astype(F32))
        if i < nb - 1:
            st[c] = s
            gs[c] = s.astype(BF16)
            g_copy(i + 1, c).start()
        else:
            a = ancv[:, cols(c)]
            new = slow_beta * momv[:, cols(c)] + (a - s) / base_rate
            gs[c] = (a - slow_rate * base_rate * new).astype(BF16)
            wy_copy(c).start()
            wc_copy(c).start()
            own_out(c).start()
            momo[c] = new
            mom_out(c).start()

    def stage_r(c):
        wy_copy(c).wait()
        wr_copy(c).start()
        far_out(c).start()

    stages = [stage_a, stage_b, stage_c]
    stages += [functools.partial(stage_g, i) for i in range(nb)]
    stages += [stage_r]
    offsets = [LAG * i for i in range(len(stages))]

    def step(t, carry):
        for stage, offset in reversed(list(zip(stages, offsets))):
            c = t - offset

            @pl.when(jnp.logical_and(c >= 0, c < chunks))
            def _():
                stage(c)

        return carry

    lax.fori_loop(0, chunks + offsets[-1], step, 0)

    def finish(c, carry):
        wc_copy(c).wait()
        wr_copy(c).wait()
        own_out(c).wait()
        far_out(c).wait()
        mom_out(c).wait()
        return carry

    lax.fori_loop(0, chunks, finish, 0)


def outer_step(mask, hidden, cotangent, anchor, momentum):
    bits = [b for b in range(5) if mask >> b & 1]
    nb = len(bits)
    tokens, h = hidden.shape[1:]
    d = cotangent.shape[2]
    rows = anchor.shape[1]
    width = WIDTH
    chunks = d // width
    block = (chunks, rows, width)
    dma = pltpu.SemaphoreType.DMA
    return pl.pallas_call(
        functools.partial(kernel, bits, chunks, width, rows),
        out_shape=(jax.ShapeDtypeStruct((1, h, d), BF16), jax.ShapeDtypeStruct((1, rows, d), F32)),
        in_specs=[pl.BlockSpec(memory_space=pl.ANY)] * 4,
        out_specs=[pl.BlockSpec(memory_space=pl.ANY)] * 2,
        scratch_shapes=[
            pltpu.VMEM((tokens, h), BF16),
            pltpu.VMEM((h, tokens), BF16),
            pltpu.VMEM((chunks, tokens, width), BF16),
            pltpu.VMEM((rows, d), F32),
            pltpu.VMEM((rows, d), F32),
            pltpu.VMEM((chunks, 2, 2, rows, width), BF16),
            pltpu.VMEM((chunks, 2, rows, width), BF16),
            pltpu.VMEM(block, BF16),
            pltpu.VMEM(block, BF16),
            pltpu.VMEM(block, F32),
            pltpu.VMEM(block, BF16),
            pltpu.VMEM((nb,) + block, BF16),
            pltpu.VMEM(block, F32),
            pltpu.VMEM(block, BF16),
            dma((3,)),
            dma((chunks,)),
            dma((3, chunks)),
            dma((5 + nb, chunks)),
            dma((5 + nb, chunks)),
        ],
        compiler_params=pltpu.CompilerParams(
            collective_id=mask, has_side_effects=True, vmem_limit_bytes=60 * 1024 * 1024),
        name=f"outer_{mask}",
    )(hidden, cotangent, anchor, momentum)


def local(hidden, cotangent, anchor, momentum, round_mask):
    branches = [functools.partial(outer_step, mask) for mask in range(1, 32)]
    return lax.switch(round_mask[0] - 1, branches, hidden, cotangent, anchor, momentum)


def solution(mesh):
    placed = (
        P("hst", "node", None),
        P("hst", "node", None),
        P("hst", "node", None),
        P("hst", "node", None),
        P(),
    )
    return jax.shard_map(
        local,
        mesh=mesh,
        in_specs=placed,
        out_specs=(P("hst", None, None), P("hst", "node", None)),
        check_vma=False,
    )
```

```python
import functools

import jax
import jax.numpy as jnp
from jax import lax
from jax.experimental import pallas as pl
from jax.experimental.pallas import tpu as pltpu
from jax.sharding import PartitionSpec as P

MESH = pl.DeviceIdType.MESH
BF16, F32 = jnp.bfloat16, jnp.float32

base_rate = 0.5
slow_rate = 1.0
slow_beta = 0.7

PART = 80
WIDTH_PAIR = 256
M_BLOCKS = 2


def flip(v, o):
    if o == 0:
        return v
    if o == 1:
        return v + 1 - 2 * lax.rem(v, 2)
    if o == 2:
        return v + 2 - 4 * lax.div(v, 2)
    return 3 - v


class Place:
    def __init__(self):
        self.node = lax.axis_index("node")
        self.hst = lax.axis_index("hst")
        self.core = lax.rem(self.node, 2)
        self.yh = lax.div(self.node, 2)
        self.yl = lax.div(self.hst, 16)
        self.y = 2 * self.yh + self.yl
        self.oc = 1 - self.core
        self.oy = 1 - self.yh
        self.mate = (2 * self.yh + self.oc, self.hst)
        self.across = (2 * self.oy + self.core, self.hst)

    def along(self, stride):
        return lax.rem(lax.div(self.hst, stride), 4)

    def hop(self, stride, o):
        v = self.along(stride)
        return (self.node, self.hst + (flip(v, o) - v) * stride)

    def hop_y(self, o):
        other = flip(self.y, o)
        return (2 * lax.div(other, 2) + self.core, self.hst + (lax.rem(other, 2) - self.yl) * 16)


def multiple(i, size):
    return pl.ds(pl.multiple_of(i * size, size), size)


def greet(partners):
    barrier = pltpu.get_barrier_semaphore()
    for who in partners:
        pl.semaphore_signal(barrier, inc=1, device_id=who, device_id_type=MESH)
    return lambda: pl.semaphore_wait(barrier, len(partners))


def load_inputs(hid, cot, anc, mom, hv, ht, cotv, ancv, momv, in_sem, cot_sem, width, chunks):
    def load_cot(c):
        return pltpu.make_async_copy(cot.at[0, :, multiple(c, width)], cotv.at[c], cot_sem.at[c])

    load_h = pltpu.make_async_copy(hid.at[0], hv, in_sem.at[0])
    load_a = pltpu.make_async_copy(anc.at[0], ancv, in_sem.at[1])
    load_m = pltpu.make_async_copy(mom.at[0], momv, in_sem.at[2])
    load_h.start()
    load_cot(0).start()
    load_m.start()
    load_a.start()

    def start_cot(c, carry):
        load_cot(c).start()
        return carry

    lax.fori_loop(1, chunks, start_cot, 0)
    load_h.wait()

    def turn(j, carry):
        ht[multiple(j, 128), :] = hv[:, multiple(j, 128)].T
        return carry

    lax.fori_loop(0, ht.shape[0] // 128, turn, 0)
    load_m.wait()
    load_a.wait()
    return load_cot


def partial_product(c, load_cot, ht, cotv, pb, rows, width, tokens):
    load_cot(c).wait()
    scale = -base_rate / (tokens * 4)
    size = ht.shape[0] // M_BLOCKS

    def block(m, carry):
        product = jnp.dot(ht[multiple(m, size), :], cotv[c], preferred_element_type=F32)
        pb[c, m] = (product * scale).astype(BF16).reshape(2, rows, width)
        return carry

    lax.fori_loop(0, M_BLOCKS, block, 0)


def run(stages, offsets, chunks):
    def step(t, carry):
        for stage, offset in reversed(list(zip(stages, offsets))):
            c = t - offset

            @pl.when(jnp.logical_and(c >= 0, c < chunks))
            def _():
                stage(c)

        return carry

    lax.fori_loop(0, chunks + offsets[-1], step, 0)


def pair_kernel(bits, lag, chunks, width, rows,
                hid, cot, anc, mom, wout, mout,
                hv, ht, cotv, ancv, momv, pb, cr, ys, yr, st, gs, gr,
                in_sem, cot_sem, send_sem, recv_sem):
    me = Place()
    core, yh, oc, oy = me.core, me.yh, me.oc, me.oy
    far = 2 * oy + core
    partners = []
    for b in bits:
        if b == 4:
            partners.append(me.hop_y(1))
        else:
            partners.append(me.hop(1 if b < 2 else 4, 1 << b % 2))
    nb = len(bits)
    K_CORE, K_Y, K_WY, K_WC, K_WR, K_G = 0, 1, 2, 3, 4, 5
    wait_all = greet([me.mate, me.across] + partners)
    load_cot = load_inputs(hid, cot, anc, mom, hv, ht, cotv, ancv, momv, in_sem, cot_sem, width, chunks)
    wait_all()

    def remote(kind, c, src, dst, who):
        return pltpu.make_async_remote_copy(
            src_ref=src, dst_ref=dst,
            send_sem=send_sem.at[kind, lax.rem(c, send_sem.shape[1])],
            recv_sem=recv_sem.at[kind, lax.rem(c, recv_sem.shape[1])],
            device_id=who, device_id_type=MESH)

    def weights(n, c):
        return wout.at[0, multiple(n, rows), multiple(c, width)]

    def core_copy(c):
        return remote(K_CORE, c, pb.at[c, :, oc], cr.at[c], me.mate)

    def y_copy(c):
        return remote(K_Y, c, ys.at[c], yr.at[c], me.across)

    def g_copy(i, c):
        return remote(K_G + i, c, gs.at[c], gr.at[i, c], partners[i])

    def wy_copy(c):
        return remote(K_WY, c, weights(me.node, c), weights(me.node, c), me.across)

    def wc_copy(c):
        return remote(K_WC, c, weights(me.node, c), weights(me.node, c), me.mate)

    def wr_copy(c):
        return remote(K_WR, c, weights(far, c), weights(far, c), me.mate)

    def by_rows(body):
        def one(r, carry):
            body(multiple(r, 32))
            return carry

        lax.fori_loop(0, rows // 32, one, 0)

    def stage_a(c):
        partial_product(c, load_cot, ht, cotv, pb, rows, width, hid.shape[1])
        core_copy(c).start()

    def stage_b(c):
        core_copy(c).wait()

        def body(r):
            ys[c, r] = (pb[c, oy, core, r].astype(F32) + cr[c, oy, r].astype(F32)).astype(BF16)

        by_rows(body)
        y_copy(c).start()

    def stage_c(c):
        y_copy(c).wait()

        def body(r):
            grad = pb[c, yh, core, r].astype(F32) + cr[c, yh, r].astype(F32) + yr[c, r].astype(F32)
            s = ancv[r, multiple(c, width)] + grad
            st[c, r] = s
            gs[c, r] = s.astype(BF16)

        by_rows(body)
        g_copy(0, c).start()

    def stage_g(i, c):
        g_copy(i, c).wait()

        def body(r):
            s = 0.5 * (st[c, r] + gr[i, c, r].astype(F32))
            st[c, r] = s
            gs[c, r] = s.astype(BF16)

        by_rows(body)
        g_copy(i + 1, c).start()

    def stage_u(c):
        g_copy(nb - 1, c).wait()

        def body(r):
            s = 0.5 * (st[c, r] + gr[nb - 1, c, r].astype(F32))
            a = ancv[r, multiple(c, width)]
            new = slow_beta * momv[r, multiple(c, width)] + (a - s) / base_rate
            mout[0, r, multiple(c, width)] = new
            here = pl.ds(pl.multiple_of(me.node * rows + r.start, 32), 32)
            wout[0, here, multiple(c, width)] = (a - slow_rate * base_rate * new).astype(BF16)

        by_rows(body)
        wy_copy(c).start()
        wc_copy(c).start()

    def stage_r(c):
        wy_copy(c).wait()
        wc_copy(c).wait()
        wr_copy(c).start()

    def stage_z(c):
        wr_copy(c).wait()

    stages = [stage_a, stage_b, stage_c]
    stages += [functools.partial(stage_g, i) for i in range(nb - 1)]
    stages += [stage_u, stage_r, stage_z]
    run(stages, [lag * i for i in range(len(stages))], chunks)


def ring_kernel(stride, group, extra, lag, chunks, width, rows,
                hid, cot, anc, mom, wout, mout,
                hv, ht, cotv, ancv, momv, pb, cr, sq, r1, st, es, er, sy, ry, av, ms, mr,
                in_sem, cot_sem, send_sem, recv_sem):
    me = Place()
    core, yh, oc, oy, y = me.core, me.yh, me.oc, me.oy, me.y
    n = len(group) + 1
    part_w = width // n
    v = me.along(stride)
    members = (lambda o: flip(v, o)) if n == 4 else (lambda o: lax.rem(lax.div(flip(v, o), group[0]), 2))
    own = members(0)
    ne = len(extra)
    first = [me.hop(stride, o) for o in group]
    swaps = [me.hop(s, o) for s, o in extra]
    ring = [me.hop_y(o) for o in (1, 2, 3)]
    hosts = 2 * n * 2**ne
    K_CORE, K_M, K_WC = 0, 1, 2
    K_R = 3
    K_E = K_R + n - 1
    K_Y = K_E + ne
    K_AY = K_Y + 3
    K_AR = K_AY + 3
    wait_all = greet([me.mate] + first + swaps + ring)
    load_cot = load_inputs(hid, cot, anc, mom, hv, ht, cotv, ancv, momv, in_sem, cot_sem, width, chunks)
    wait_all()

    def remote(kind, c, src, dst, who):
        return pltpu.make_async_remote_copy(
            src_ref=src, dst_ref=dst,
            send_sem=send_sem.at[kind, lax.rem(c, send_sem.shape[1])],
            recv_sem=recv_sem.at[kind, lax.rem(c, recv_sem.shape[1])],
            device_id=who, device_id_type=MESH)

    def core_copy(c):
        return remote(K_CORE, c, pb.at[c, :, oc], cr.at[c], me.mate)

    def mom_copy(c):
        return remote(K_M, c, ms.at[c], mr.at[c], me.across)

    def r_copy(i, c):
        return remote(K_R + i, c, sq.at[c, members(group[i])], r1.at[c, i], first[i])

    def e_copy(i, c):
        return remote(K_E + i, c, es.at[c], er.at[i, c], swaps[i])

    def y_copy(i, c):
        return remote(K_Y + i, c, sy.at[c, flip(y, i + 1)], ry.at[c, i], ring[i])

    def ay_copy(i, c):
        return remote(K_AY + i, c, av.at[c, own, y], av.at[c, own, y], ring[i])

    def ar_copy(i, c):
        return remote(K_AR + i, c, av.at[c, own], av.at[c, own], first[i])

    def weights(h, c):
        return wout.at[0, multiple(2 * h + core, rows), multiple(c, width)]

    def wc_copy(h, c):
        return remote(K_WC + (K_AR + n - 1 - K_WC) * h, c, weights(h, c), weights(h, c), me.mate)

    def quarters(body):
        def one(q, carry):
            body(q)
            return carry

        lax.fori_loop(0, 4, one, 0)

    def stage_a(c):
        partial_product(c, load_cot, ht, cotv, pb, rows, width, hid.shape[1])
        core_copy(c).start()

        def body(r, carry):
            ms[c, multiple(r, PART)] = momv[multiple(r, PART), multiple(c, width)].astype(BF16)
            return carry

        lax.fori_loop(0, 2, body, 0)
        mom_copy(c).start()

    def stage_b(c):
        core_copy(c).wait()
        mom_copy(c).wait()

        def body(q):
            h, r = lax.div(q, 2), multiple(lax.rem(q, 2), PART)
            s = pb[c, h, core, r].astype(F32) + cr[c, h, r].astype(F32)
            s = s + jnp.where(h == yh, ancv[r, multiple(c, width)], 0.0)
            s = s.astype(BF16)
            for j in range(n):
                sq[c, j, q] = s[:, j * part_w:(j + 1) * part_w]

        quarters(body)
        for i in range(n - 1):
            r_copy(i, c).start()

    def send_on(i, c):
        if i < ne:
            e_copy(i, c).start()
        else:
            for o in range(3):
                y_copy(o, c).start()

    def keep(i, c, q, s):
        if i < ne:
            st[c, q] = s
            es[c, q] = s.astype(BF16)
        else:
            sy[c, q] = s.astype(BF16)

    def stage_r(c):
        for i in range(n - 1):
            r_copy(i, c).wait()

        def body(q):
            s = sq[c, own, q].astype(F32)
            for i in range(n - 1):
                s = s + r1[c, i, q].astype(F32)
            keep(0, c, q, s)

        quarters(body)
        send_on(0, c)

    def stage_e(i, c):
        e_copy(i, c).wait()
        quarters(lambda q: keep(i + 1, c, q, st[c, q] + er[i, c, q].astype(F32)))
        send_on(i + 1, c)

    def stage_f(c):
        for i in range(3):
            y_copy(i, c).wait()
        s = sy[c, y].astype(F32) + ry[c, 0].astype(F32) + ry[c, 1].astype(F32) + ry[c, 2].astype(F32)
        av[c, own, y] = (s * (1.0 / hosts)).astype(BF16)
        for i in range(3):
            ay_copy(i, c).start()

    def stage_g(c):
        for i in range(3):
            ay_copy(i, c).wait()
        for i in range(n - 1):
            ar_copy(i, c).start()

    def stage_u(c):
        for i in range(n - 1):
            ar_copy(i, c).wait()

        def body(p, carry):
            r = multiple(p, PART)
            for j in range(n):
                w = pl.ds(pl.multiple_of(c * width + j * part_w, part_w), part_w)
                a = ancv[r, w]
                new = slow_beta * momv[r, w] + (a - av[c, j, 2 * yh + p].astype(F32)) / base_rate
                mout[0, r, w] = new
                here = pl.ds(pl.multiple_of((2 * yh + core) * rows + p * PART, PART), PART)
                there = pl.ds(pl.multiple_of((2 * oy + core) * rows + p * PART, PART), PART)
                wout[0, here, w] = (a - slow_rate * base_rate * new).astype(BF16)
                shift = mr[c, r, pl.ds(j * part_w, part_w)].astype(F32) * (slow_rate * base_rate * slow_beta)
                wout[0, there, w] = (av[c, j, 2 * oy + p].astype(F32) - shift).astype(BF16)
            return carry

        lax.fori_loop(0, 2, body, 0)
        wc_copy(0, c).start()
        wc_copy(1, c).start()

    def stage_z(c):
        wc_copy(0, c).wait()
        wc_copy(1, c).wait()

    stages = [stage_a, stage_b, stage_r]
    stages += [functools.partial(stage_e, i) for i in range(ne)]
    stages += [stage_f, stage_g, stage_u, stage_z]
    run(stages, [lag * i for i in range(len(stages))], chunks)


def outer_step(mask, hidden, cotangent, anchor, momentum):
    tokens, h = hidden.shape[1:]
    d = cotangent.shape[2]
    rows = anchor.shape[1]
    dma = pltpu.SemaphoreType.DMA
    lowest = mask & 15
    if mask & 16 and lowest:
        z, x = mask & 3, mask >> 2 & 3
        stride, value, other, rest = (4, x, 1, z) if x == 3 or not z or (z != 3 and x) else (1, z, 4, x)
        group = (1, 2, 3) if value == 3 else (value,)
        extra = [(other, o) for o in (1, 2) if rest & o]
        n, ne = len(group) + 1, len(extra)
        width = 128 * max(n, 2)
        chunks = d // width
        lag = 3 if n == 2 else 2
        part_w = width // n
        piece = (4, PART, part_w)
        body = functools.partial(ring_kernel, stride, group, extra, lag, chunks, width, rows)
        kinds = 3 + 2 * (n - 1) + ne + 6 + 1
        scratch = [
            pltpu.VMEM((chunks, n) + piece, BF16),
            pltpu.VMEM((chunks, n - 1) + piece, BF16),
            pltpu.VMEM((chunks if ne else 1,) + piece, F32),
            pltpu.VMEM((chunks if ne else 1,) + piece, BF16),
            pltpu.VMEM((max(ne, 1), chunks if ne else 1) + piece, BF16),
            pltpu.VMEM((chunks,) + piece, BF16),
            pltpu.VMEM((chunks, 3, PART, part_w), BF16),
            pltpu.VMEM((chunks, n) + piece, BF16),
            pltpu.VMEM((chunks, rows, width), BF16),
            pltpu.VMEM((chunks, rows, width), BF16),
        ]
    else:
        bits = [b for b in range(5) if mask >> b & 1]
        nb = len(bits)
        width = WIDTH_PAIR
        chunks = d // width
        lag = 3 if nb <= 2 else 2
        block = (chunks, rows, width)
        body = functools.partial(pair_kernel, bits, lag, chunks, width, rows)
        kinds = 5 + nb
        scratch = [
            pltpu.VMEM(block, BF16),
            pltpu.VMEM(block, BF16),
            pltpu.VMEM(block, F32),
            pltpu.VMEM(block, BF16),
            pltpu.VMEM((nb,) + block, BF16),
        ]
    return pl.pallas_call(
        body,
        out_shape=(jax.ShapeDtypeStruct((1, h, d), BF16), jax.ShapeDtypeStruct((1, rows, d), F32)),
        in_specs=[pl.BlockSpec(memory_space=pltpu.HBM)] * 4,
        out_specs=[pl.BlockSpec(memory_space=pltpu.VMEM)] * 2,
        scratch_shapes=[
            pltpu.VMEM((tokens, h), BF16),
            pltpu.VMEM((h, tokens), BF16),
            pltpu.VMEM((chunks, tokens, width), BF16),
            pltpu.VMEM((rows, d), F32),
            pltpu.VMEM((rows, d), F32),
            pltpu.VMEM((chunks, 2, 2, rows, width), BF16),
            pltpu.VMEM((chunks, 2, rows, width), BF16),
        ] + scratch + [
            dma((3,)),
            dma((chunks,)),
            dma((kinds, lag)),
            dma((kinds, 2 * lag)),
        ],
        compiler_params=pltpu.CompilerParams(
            collective_id=mask, has_side_effects=True, vmem_limit_bytes=VMEM_LIMIT),
        name=f"outer_{mask}",
    )(hidden, cotangent, anchor, momentum)


VMEM_LIMIT = 54 * 1024 * 1024
MASKS = range(1, 32)


def local(hidden, cotangent, anchor, momentum, round_mask):
    branches = [functools.partial(outer_step, mask) for mask in MASKS]
    return lax.switch(round_mask[0] - 1, branches, hidden, cotangent, anchor, momentum)


def solution(mesh):
    placed = (
        P("hst", "node", None),
        P("hst", "node", None),
        P("hst", "node", None),
        P("hst", "node", None),
        P(),
    )
    return jax.shard_map(
        local,
        mesh=mesh,
        in_specs=placed,
        out_specs=(P("hst", None, None), P("hst", "node", None)),
        check_vma=False,
    )
```

```python
import functools

import jax
import jax.numpy as jnp
from jax import lax
from jax.experimental import pallas as pl
from jax.experimental.pallas import tpu as pltpu
from jax.sharding import PartitionSpec as P

MESH = pl.DeviceIdType.MESH
BF16, F32 = jnp.bfloat16, jnp.float32

base_rate = 0.5
slow_rate = 1.0
slow_beta = 0.7

PART = 80
WIDTH_PAIR = 256
M_BLOCKS = 4


def flip(v, o):
    if o == 0:
        return v
    if o == 1:
        return v + 1 - 2 * lax.rem(v, 2)
    if o == 2:
        return v + 2 - 4 * lax.div(v, 2)
    return 3 - v


class Place:
    def __init__(self):
        self.node = lax.axis_index("node")
        self.hst = lax.axis_index("hst")
        self.core = lax.rem(self.node, 2)
        self.yh = lax.div(self.node, 2)
        self.yl = lax.div(self.hst, 16)
        self.y = 2 * self.yh + self.yl
        self.oc = 1 - self.core
        self.oy = 1 - self.yh
        self.mate = (2 * self.yh + self.oc, self.hst)
        self.across = (2 * self.oy + self.core, self.hst)

    def along(self, stride):
        return lax.rem(lax.div(self.hst, stride), 4)

    def hop(self, stride, o):
        v = self.along(stride)
        return (self.node, self.hst + (flip(v, o) - v) * stride)

    def hop_y(self, o):
        other = flip(self.y, o)
        return (2 * lax.div(other, 2) + self.core, self.hst + (lax.rem(other, 2) - self.yl) * 16)


def blend(a, b, p):
    return a if a is b else a + (b - a) * p


def multiple(i, size):
    return pl.ds(pl.multiple_of(i * size, size), size)


def greet(partners):
    barrier = pltpu.get_barrier_semaphore()
    for who in partners:
        pl.semaphore_signal(barrier, inc=1, device_id=who, device_id_type=MESH)
    return lambda: pl.semaphore_wait(barrier, len(partners))


def load_inputs(hid, cot, anc, mom, hv, ht, cotv, ancv, momv, in_sem, cot_sem, width, chunks):
    def load_cot(c):
        return pltpu.make_async_copy(cot.at[0, :, multiple(c, width)], cotv.at[c], cot_sem.at[c])

    load_h = pltpu.make_async_copy(hid.at[0], hv, in_sem.at[0])
    load_a = pltpu.make_async_copy(anc.at[0], ancv, in_sem.at[1])
    load_m = pltpu.make_async_copy(mom.at[0], momv, in_sem.at[2])
    load_h.start()
    load_cot(0).start()
    load_m.start()
    load_a.start()

    def start_cot(c, carry):
        load_cot(c).start()
        return carry

    lax.fori_loop(1, chunks, start_cot, 0)
    load_h.wait()

    def turn(j, carry):
        ht[multiple(j, 128), :] = hv[:, multiple(j, 128)].T
        return carry

    lax.fori_loop(0, ht.shape[0] // 128, turn, 0)
    load_m.wait()
    load_a.wait()
    return load_cot


def partial_product(c, load_cot, ht, cotv, pb, rows, width, tokens):
    load_cot(c).wait()
    scale = -base_rate / (tokens * 4)
    size = ht.shape[0] // M_BLOCKS

    def block(m, carry):
        product = jnp.dot(ht[multiple(m, size), :], cotv[c], preferred_element_type=F32)
        pb[c, lax.div(m, 2), lax.rem(m, 2)] = (product * scale).astype(BF16).reshape(rows, width)
        return carry

    lax.fori_loop(0, M_BLOCKS, block, 0)


def out_copy(wv, wout, out_sem, width, c):
    return pltpu.make_async_copy(
        wv.at[:, multiple(c, width)], wout.at[0, :, multiple(c, width)], out_sem.at[lax.rem(c, out_sem.shape[0])])


def run(stages, offsets, chunks):
    def step(t, carry):
        for stage, offset in reversed(list(zip(stages, offsets))):
            c = t - offset

            @pl.when(jnp.logical_and(c >= 0, c < chunks))
            def _():
                stage(c)

        return carry

    lax.fori_loop(0, chunks + offsets[-1], step, 0)


def pair_kernel(bits, lag, chunks, width, rows,
                hid, cot, anc, mom, wout, mout,
                hv, ht, cotv, ancv, momv, pb, cr, wv, ys, yr, st, gs, gr,
                in_sem, cot_sem, out_sem, send_sem, recv_sem):
    me = Place()
    core, yh, oc, oy = me.core, me.yh, me.oc, me.oy
    far = 2 * oy + core
    partners = []
    for b in bits:
        if b == 4:
            partners.append(me.hop_y(1))
        else:
            partners.append(me.hop(1 if b < 2 else 4, 1 << b % 2))
    nb = len(bits)
    K_CORE, K_Y, K_WY, K_WC, K_WR, K_G = 0, 1, 2, 3, 4, 5
    wait_all = greet([me.mate, me.across] + partners)
    load_cot = load_inputs(hid, cot, anc, mom, hv, ht, cotv, ancv, momv, in_sem, cot_sem, width, chunks)
    wait_all()

    def remote(kind, c, src, dst, who):
        return pltpu.make_async_remote_copy(
            src_ref=src, dst_ref=dst,
            send_sem=send_sem.at[kind, lax.rem(c, send_sem.shape[1])],
            recv_sem=recv_sem.at[kind, lax.rem(c, recv_sem.shape[1])],
            device_id=who, device_id_type=MESH)

    def weights(n, c):
        return wv.at[multiple(n, rows), multiple(c, width)]

    def core_copy(c):
        return remote(K_CORE, c, pb.at[c, :, oc], cr.at[c], me.mate)

    def y_copy(c):
        return remote(K_Y, c, ys.at[c], yr.at[c], me.across)

    def g_copy(i, c):
        return remote(K_G + i, c, gs.at[c], gr.at[i, c], partners[i])

    def wy_copy(c):
        return remote(K_WY, c, weights(me.node, c), weights(me.node, c), me.across)

    def wc_copy(c):
        return remote(K_WC, c, weights(me.node, c), weights(me.node, c), me.mate)

    def wr_copy(c):
        return remote(K_WR, c, weights(far, c), weights(far, c), me.mate)

    def by_rows(body):
        def one(r, carry):
            body(multiple(r, 32))
            return carry

        lax.fori_loop(0, rows // 32, one, 0)

    def stage_a(c):
        partial_product(c, load_cot, ht, cotv, pb, rows, width, hid.shape[1])
        core_copy(c).start()

    def stage_b(c):
        core_copy(c).wait()

        def body(r):
            ys[c, r] = (pb[c, oy, core, r].astype(F32) + cr[c, oy, r].astype(F32)).astype(BF16)

        by_rows(body)
        y_copy(c).start()

    def stage_c(c):
        y_copy(c).wait()

        def body(r):
            grad = pb[c, yh, core, r].astype(F32) + cr[c, yh, r].astype(F32) + yr[c, r].astype(F32)
            s = ancv[r, multiple(c, width)] + grad
            st[c, r] = s
            gs[c, r] = s.astype(BF16)

        by_rows(body)
        g_copy(0, c).start()

    def stage_g(i, c):
        g_copy(i, c).wait()

        def body(r):
            s = 0.5 * (st[c, r] + gr[i, c, r].astype(F32))
            st[c, r] = s
            gs[c, r] = s.astype(BF16)

        by_rows(body)
        g_copy(i + 1, c).start()

    def stage_u(c):
        g_copy(nb - 1, c).wait()

        def body(r):
            s = 0.5 * (st[c, r] + gr[nb - 1, c, r].astype(F32))
            a = ancv[r, multiple(c, width)]
            new = slow_beta * momv[r, multiple(c, width)] + (a - s) / base_rate
            mout[0, r, multiple(c, width)] = new
            here = pl.ds(pl.multiple_of(me.node * rows + r.start, 32), 32)
            wv[here, multiple(c, width)] = (a - slow_rate * base_rate * new).astype(BF16)

        by_rows(body)
        wy_copy(c).start()
        wc_copy(c).start()

    def stage_r(c):
        wy_copy(c).wait()
        wc_copy(c).wait()
        wr_copy(c).start()

    def stage_z(c):
        wr_copy(c).wait()
        out_copy(wv, wout, out_sem, width, c).start()

    def stage_end(c):
        out_copy(wv, wout, out_sem, width, c).wait()

    stages = [stage_a, stage_b, stage_c]
    stages += [functools.partial(stage_g, i) for i in range(nb - 1)]
    stages += [stage_u, stage_r, stage_z, stage_end]
    run(stages, [lag * i for i in range(len(stages))], chunks)


def ring_kernel(plan, lag, chunks, width, rows,
                hid, cot, anc, mom, wout, mout,
                hv, ht, cotv, ancv, momv, pb, cr, wv, sq, r1, st, es, er, sq2, r2, sy, ry, av, mr,
                in_sem, cot_sem, out_sem, send_sem, recv_sem):
    ring_all, plans = plan
    me = Place()
    core, yh, oc, oy = me.core, me.yh, me.oc, me.oy
    group, second, extra = plans[0][1:]
    n, n2, ne = len(group) + 1, 2 if second else 1, len(extra)
    part_w = width // (n * n2)
    offsets_y = (1, 2, 3) if ring_all else (2,)
    ny = len(offsets_y) + 1
    quads = 4 // ny
    mine_y = me.y if ring_all else yh
    hosts = n * n2 * 2**ne * (2 if ring_all else 1)
    alike = plans[0] == plans[1]

    def both(make):
        a = make(plans[0])
        return (a, a) if alike else (a, make(plans[1]))

    def place_in(stride, size, bit, o):
        v = flip(me.along(stride), o)
        return v if size == 4 else lax.rem(lax.div(v, bit), 2)

    def hop(pick):
        return both(lambda p: me.hop(*pick(p))[1])

    first = [hop(lambda p, i=i: (p[0], p[1][i])) for i in range(n - 1)]
    theirs = [both(lambda p, i=i: place_in(p[0], n, p[1][0], p[1][i])) for i in range(n - 1)]
    own_all = both(lambda p: place_in(p[0], n, p[1][0], 0))
    partner2 = hop(lambda p: p[2]) if second else None
    own2_all = both(lambda p: place_in(p[2][0], 2, p[2][1], 0)) if second else (0, 0)
    swaps = [hop(lambda p, i=i: p[3][i]) for i in range(ne)]
    ring = [me.hop_y(o) for o in offsets_y]
    K_CORE, K_M, K_WC, K_S, K_AS = 0, 1, 2, 4, 5
    K_M2 = 6
    K_R = 7
    K_E = K_R + n - 1
    K_Y = K_E + ne
    K_AY = K_Y + ny - 1
    K_AR = K_AY + ny - 1
    ids = [a for a, _ in first]
    if second:
        ids += [partner2[0]]
    elif alike:
        ids += [a for a, _ in swaps]
    else:
        ids += [b for _, b in first]
    ids = [(me.node, i) for i in ids]
    wait_all = greet([me.mate] + ids + ring)
    load_cot = load_inputs(hid, cot, anc, mom, hv, ht, cotv, ancv, momv, in_sem, cot_sem, width, chunks)
    wait_all()

    def at(pair, c):
        return blend(pair[0], pair[1], lax.rem(c, 2))

    def remote(kind, c, src, dst, who):
        return pltpu.make_async_remote_copy(
            src_ref=src, dst_ref=dst,
            send_sem=send_sem.at[kind, lax.rem(c, send_sem.shape[1])],
            recv_sem=recv_sem.at[kind, lax.rem(c, recv_sem.shape[1])],
            device_id=who, device_id_type=MESH)

    def core_copy(c):
        return remote(K_CORE, c, pb.at[c, :, oc], cr.at[c], me.mate)

    def mom_copy(half, c):
        r = pl.ds(half * PART, PART)
        return remote(K_M2 if half else K_M, c, pb.at[c, 0, oc, r], mr.at[c, r], me.across)

    def r_copy(i, c):
        return remote(K_R + i, c, sq.at[c, at(theirs[i], c)], r1.at[c, i], (me.node, at(first[i], c)))

    def s_copy(c):
        return remote(K_S, c, sq2.at[c, 1 - at(own2_all, c)], r2.at[c], (me.node, at(partner2, c)))

    def as_copy(c):
        part = av.at[c, at(own_all, c), at(own2_all, c)]
        return remote(K_AS, c, part, part, (me.node, at(partner2, c)))

    def e_copy(i, c):
        return remote(K_E + i, c, es.at[c], er.at[i, c], (me.node, at(swaps[i], c)))

    def piece(m):
        return pl.ds(m * quads, quads)

    def y_copy(i, c):
        theirs_y = flip(me.y, i + 1) if ring_all else oy
        return remote(K_Y + i, c, sy.at[c, piece(theirs_y)], ry.at[c, i], ring[i])

    def ay_copy(i, c):
        part = av.at[c, at(own_all, c), at(own2_all, c), piece(mine_y)]
        return remote(K_AY + i, c, part, part, ring[i])

    def ar_copy(i, c):
        part = av.at[c, at(own_all, c)]
        return remote(K_AR + i, c, part, part, (me.node, at(first[i], c)))

    def weights(h, c):
        return wv.at[multiple(2 * h + core, rows), multiple(c, width)]

    def wc_copy(h, c):
        return remote(K_WC + h, c, weights(h, c), weights(h, c), me.mate)

    def quarters(body):
        def one(q, carry):
            body(q)
            return carry

        lax.fori_loop(0, 4, one, 0)

    def stage_a(c):
        partial_product(c, load_cot, ht, cotv, pb, rows, width, hid.shape[1])
        core_copy(c).start()

    def stage_b(c):
        core_copy(c).wait()

        def body(q):
            h, r = lax.div(q, 2), multiple(lax.rem(q, 2), PART)
            s = pb[c, h, core, r].astype(F32) + cr[c, h, r].astype(F32)
            s = s + jnp.where(h == yh, ancv[r, multiple(c, width)], 0.0)
            s = s.astype(BF16)
            for j in range(n):
                for k in range(n2):
                    sq[c, j, k, q] = s[:, (j * n2 + k) * part_w:(j * n2 + k + 1) * part_w]

        quarters(body)
        for i in range(n - 1):
            r_copy(i, c).start()

        def shift(r, carry):
            pb[c, 0, oc, multiple(r, PART)] = momv[multiple(r, PART), multiple(c, width)].astype(BF16)
            return carry

        lax.fori_loop(0, 2, shift, 0)
        mom_copy(0, c).start()

    def send_on(i, c):
        if i < ne:
            e_copy(i, c).start()
        else:
            for o in range(ny - 1):
                y_copy(o, c).start()

    def keep(i, c, q, s):
        if i < ne:
            st[c, q] = s
            es[c, q] = s.astype(BF16)
        else:
            sy[c, q] = s.astype(BF16)

    def stage_r(c):
        for i in range(n - 1):
            r_copy(i, c).wait()
        mom_copy(0, c).wait()
        own = at(own_all, c)

        def body(q):
            for k in range(n2):
                s = sq[c, own, k, q].astype(F32)
                for i in range(n - 1):
                    s = s + r1[c, i, k, q].astype(F32)
                if second:
                    sq2[c, k, q] = s.astype(BF16)
                else:
                    keep(0, c, q, s)

        quarters(body)
        if second:
            s_copy(c).start()
        else:
            send_on(0, c)

    def stage_s(c):
        s_copy(c).wait()
        own2 = at(own2_all, c)
        quarters(lambda q: keep(0, c, q, sq2[c, own2, q].astype(F32) + r2[c, q].astype(F32)))
        send_on(0, c)

    def stage_e(i, c):
        e_copy(i, c).wait()
        quarters(lambda q: keep(i + 1, c, q, st[c, q] + er[i, c, q].astype(F32)))
        send_on(i + 1, c)

    def stage_f(c):
        for i in range(ny - 1):
            y_copy(i, c).wait()
        own, own2 = at(own_all, c), at(own2_all, c)
        for k in range(quads):
            s = sy[c, mine_y * quads + k].astype(F32)
            for i in range(ny - 1):
                s = s + ry[c, i, k].astype(F32)
            av[c, own, own2, mine_y * quads + k] = (s * (1.0 / hosts)).astype(BF16)
        for i in range(ny - 1):
            ay_copy(i, c).start()

    def stage_g(c):
        for i in range(ny - 1):
            ay_copy(i, c).wait()
        if second:
            as_copy(c).start()
        else:
            send_back(c)

    def send_back(c):
        for i in range(n - 1):
            ar_copy(i, c).start()
        mom_copy(1, c).start()

    def stage_h(c):
        as_copy(c).wait()
        send_back(c)

    def stage_u(c):
        for i in range(n - 1):
            ar_copy(i, c).wait()
        mom_copy(1, c).wait()

        def body(p, carry):
            r = multiple(p, PART)
            here = pl.ds(pl.multiple_of((2 * yh + core) * rows + p * PART, PART), PART)
            there = pl.ds(pl.multiple_of((2 * oy + core) * rows + p * PART, PART), PART)
            for j in range(n):
                for k in range(n2):
                    at_w = (j * n2 + k) * part_w
                    w = pl.ds(pl.multiple_of(c * width + at_w, part_w), part_w)
                    a = ancv[r, w]
                    new = slow_beta * momv[r, w] + (a - av[c, j, k, 2 * yh + p].astype(F32)) / base_rate
                    mout[0, r, w] = new
                    wv[here, w] = (a - slow_rate * base_rate * new).astype(BF16)
                    shift = mr[c, r, pl.ds(at_w, part_w)].astype(F32) * (slow_rate * base_rate * slow_beta)
                    wv[there, w] = (av[c, j, k, 2 * oy + p].astype(F32) - shift).astype(BF16)
            return carry

        lax.fori_loop(0, 2, body, 0)
        wc_copy(0, c).start()
        wc_copy(1, c).start()

    def stage_z(c):
        wc_copy(0, c).wait()
        wc_copy(1, c).wait()
        out_copy(wv, wout, out_sem, width, c).start()

    def stage_end(c):
        out_copy(wv, wout, out_sem, width, c).wait()

    stages = [stage_a, stage_b, stage_r]
    stages += [stage_s] if second else []
    stages += [functools.partial(stage_e, i) for i in range(ne)]
    stages += [stage_f, stage_g]
    stages += [stage_h] if second else []
    stages += [stage_u, stage_z, stage_end]
    run(stages, [lag * i for i in range(len(stages))], chunks)


def plan_of(mask):
    z, x, ring_all = mask & 3, mask >> 2 & 3, bool(mask & 16)
    if x in (1, 2) and z in (1, 2):
        return ring_all, ((4, (x,), (1, z), ()), (1, (z,), (4, x), ()))
    if x == 3 and z == 3:
        swaps = [tuple((stride, o) for o in (1, 2)) for stride in (1, 4)]
        return ring_all, ((4, (1, 2, 3), None, swaps[0]), (1, (1, 2, 3), None, swaps[1]))
    one = None
    if x == 3 and (z or ring_all):
        one = (4, (1, 2, 3), None, ((1, z),) if z else ())
    elif z == 3 and (x or ring_all):
        one = (1, (1, 2, 3), None, ((4, x),) if x else ())
    elif ring_all and (x or z):
        one = (4, (x,), None, ()) if x else (1, (z,), None, ())
    return one and (ring_all, (one, one))


def outer_step(mask, hidden, cotangent, anchor, momentum):
    tokens, h = hidden.shape[1:]
    d = cotangent.shape[2]
    rows = anchor.shape[1]
    dma = pltpu.SemaphoreType.DMA
    plan = plan_of(mask)
    if plan:
        ring_all, (_, group, second, extra) = plan[0], plan[1][0]
        n, n2, ne = len(group) + 1, 2 if second else 1, len(extra)
        width = 128 * n * n2
        chunks = d // width
        lag = 3 if n * n2 == 2 else 2
        ny = 4 if ring_all else 2
        piece = (4, PART, 128)
        body = functools.partial(ring_kernel, plan, lag, chunks, width, rows)
        kinds = 7 + 2 * (n - 1) + ne + 2 * (ny - 1)
        some_e, some_2 = (chunks if ne else 1), (chunks if second else 1)
        scratch = [
            pltpu.VMEM((chunks, n, n2) + piece, BF16),
            pltpu.VMEM((chunks, n - 1, n2) + piece, BF16),
            pltpu.VMEM((some_e,) + piece, F32),
            pltpu.VMEM((some_e,) + piece, BF16),
            pltpu.VMEM((max(ne, 1), some_e) + piece, BF16),
            pltpu.VMEM((some_2, 2) + piece, BF16),
            pltpu.VMEM((some_2,) + piece, BF16),
            pltpu.VMEM((chunks,) + piece, BF16),
            pltpu.VMEM((chunks, ny - 1, 4 // ny, PART, 128), BF16),
            pltpu.VMEM((chunks, n, n2) + piece, BF16),
            pltpu.VMEM((chunks, rows, width), BF16),
        ]
    else:
        bits = [b for b in range(5) if mask >> b & 1]
        nb = len(bits)
        width = WIDTH_PAIR
        chunks = d // width
        lag = 3 if nb <= 2 else 2
        block = (chunks, rows, width)
        body = functools.partial(pair_kernel, bits, lag, chunks, width, rows)
        kinds = 5 + nb
        scratch = [
            pltpu.VMEM(block, BF16),
            pltpu.VMEM(block, BF16),
            pltpu.VMEM(block, F32),
            pltpu.VMEM(block, BF16),
            pltpu.VMEM((nb,) + block, BF16),
        ]
    return pl.pallas_call(
        body,
        out_shape=(jax.ShapeDtypeStruct((1, h, d), BF16), jax.ShapeDtypeStruct((1, rows, d), F32)),
        in_specs=[pl.BlockSpec(memory_space=pltpu.HBM)] * 4,
        out_specs=[pl.BlockSpec(memory_space=pltpu.HBM), pl.BlockSpec(memory_space=pltpu.VMEM)],
        scratch_shapes=[
            pltpu.VMEM((tokens, h), BF16),
            pltpu.VMEM((h, tokens), BF16),
            pltpu.VMEM((chunks, tokens, width), BF16),
            pltpu.VMEM((rows, d), F32),
            pltpu.VMEM((rows, d), F32),
            pltpu.VMEM((chunks, 2, 2, rows, width), BF16),
            pltpu.VMEM((chunks, 2, rows, width), BF16),
            pltpu.VMEM((h, d), BF16),
        ] + scratch + [
            dma((3,)),
            dma((chunks,)),
            dma((lag,)),
            dma((kinds, lag)),
            dma((kinds, 2 * lag)),
        ],
        compiler_params=pltpu.CompilerParams(
            collective_id=mask, has_side_effects=True, vmem_limit_bytes=VMEM_LIMIT),
        name=f"outer_{mask}",
    )(hidden, cotangent, anchor, momentum)


VMEM_LIMIT = 54 * 1024 * 1024
MASKS = range(1, 32)


def local(hidden, cotangent, anchor, momentum, round_mask):
    branches = [functools.partial(outer_step, mask) for mask in MASKS]
    return lax.switch(round_mask[0] - 1, branches, hidden, cotangent, anchor, momentum)


def solution(mesh):
    placed = (
        P("hst", "node", None),
        P("hst", "node", None),
        P("hst", "node", None),
        P("hst", "node", None),
        P(),
    )
    return jax.shard_map(
        local,
        mesh=mesh,
        in_specs=placed,
        out_specs=(P("hst", None, None), P("hst", "node", None)),
        check_vma=False,
    )
```
